256 devices in a mesh: store: 32 (over y, z), tp: 8 (over x, core).
Axes of the slice: x: 4, y: 4, z: 8, core: 2. Of those that a mesh axis runs over, the one named last changes fastest.
Arguments:
- queries: bfloat16 [32768, 8192], P('store', 'tp')
- fresh_kv: bfloat16 [2, 32768, 1024], P(None, ('store', 'tp'))
- page_pool: bfloat16 [2048, 2, 128, 1024], P('store', None, None, 'tp')
- page_host: int32 [128, 8], P('store'), may hold values from 0 to 31, as said below
- page_slot: int32 [128, 8], P('store'), may hold values from 0 to 63, as said below
- prefix_len: int32 [128], P('store'), may hold values from 513 to 1024
- fresh_len: int32 [32, 4], P('store'), may hold values from 1 to 384, 1024 in all within a row
Outputs:
- attention: bfloat16 [32768, 8192], P('store', 'tp')
The draws below stay inside these ranges and needn't reach their ends.
Inputs may be any that keep to these rules, and one draw needn't show every extreme that they name: `page_host`: page p of request r is read only if p < ceil(prefix_len[r] / 128). Among the pages read by the 4 requests of one host, at most 2 lie on any one host; in every draw some host holds exactly 2 of the pages read by each host. `page_slot`: several entries may name the same stored page. `fresh_len`: the requests of a host own consecutive rows of its block, in order.
All inputs are finite; a program needn't handle non-finite values.
Results may differ from the reference program's by a relative error of at most 0.0041.
Values may be sent and summed in bfloat16 or wider, within the bound.
A program may use at most 128 MiB of HBM per device.

```python
import math
import jax
import jax.numpy as jnp
import numpy as np
from jax import lax

QH = 64
KVH = 8
HD = 128
TOK_HOST = 1024
REQ_HOST = 4
PAGE = 128
PAGES_MAX = 8
SLOTS = 64
MOST_NEW = 384
CAP = 2
TOKENS = 32768
REQS = 128
N_STORE = 32


def host_table(host_key, host_id, hot_host):
    subkeys = jax.random.split(host_key, 6)
    entry_count = REQ_HOST * PAGES_MAX
    host_count = REQS // REQ_HOST
    fewest = PAGES_MAX * 5 // 8
    page_count = jax.random.randint(subkeys[0], (REQ_HOST,), fewest, PAGES_MAX + 1)
    filled = jax.random.randint(subkeys[1], (REQ_HOST,), 1, PAGE + 1)
    is_hot = host_id == hot_host
    page_count = page_count.at[0].set(jnp.where(is_hot, PAGES_MAX, page_count[0]))
    filled = filled.at[0].set(jnp.where(is_hot, PAGE, filled[0]))
    page_count = page_count.at[1].set(jnp.where(is_hot, fewest, page_count[1]))
    filled = filled.at[1].set(jnp.where(is_hot, 1, filled[1]))
    prefix = (page_count - 1) * PAGE + filled
    in_use = (jnp.arange(PAGES_MAX)[None, :] < page_count[:, None]).reshape(entry_count)
    shuffle = jax.random.permutation(subkeys[2], entry_count)
    ordering = jnp.argsort(jnp.where(in_use, 0, entry_count) + shuffle)
    entry_rank = jnp.argsort(ordering)
    grid_size = host_count * CAP
    grid_shuffle = jax.random.permutation(subkeys[3], grid_size)
    grid_owner = jnp.arange(grid_size) // CAP
    grid_order = jnp.argsort(jnp.where(grid_owner == hot_host, grid_shuffle - grid_size, grid_shuffle))
    placed = grid_order[jnp.minimum(entry_rank, grid_size - 1)] // CAP
    owners = jnp.where(in_use, placed, jax.random.randint(subkeys[4], (entry_count,), 0, host_count))
    slot_ids = jax.random.randint(subkeys[5], (entry_count,), 0, SLOTS)
    return (owners.reshape(REQ_HOST, PAGES_MAX), slot_ids.reshape(REQ_HOST, PAGES_MAX), prefix)


def page_tables(key):
    base_key = jax.random.fold_in(key, 901)
    host_count = REQS // REQ_HOST
    hot_host = jax.random.randint(jax.random.fold_in(base_key, 1), (), 0, host_count)
    host_keys = jax.random.split(jax.random.fold_in(base_key, 2), host_count)
    owners, slot_ids, prefix = jax.vmap(host_table, in_axes=(0, 0, None))(host_keys, jnp.arange(host_count), hot_host)
    return (owners.reshape(REQS, PAGES_MAX).astype(jnp.int32), slot_ids.reshape(REQS, PAGES_MAX).astype(jnp.int32), prefix.reshape(REQS).astype(jnp.int32))


def draw_page_host(key, part):
    return page_tables(key)[0]


def draw_page_slot(key, part):
    return page_tables(key)[1]


def draw_prefix_len(key, part):
    return page_tables(key)[2]


def draw_queries(key, part):
    values = jnp.clip(jax.random.normal(jax.random.fold_in(key, 911), (TOKENS, QH * HD), jnp.float32), -6.0, 6.0)
    values = values * 1.5
    return values.astype(jnp.bfloat16)


def draw_fresh_kv(key, part):
    values = jnp.clip(jax.random.normal(jax.random.fold_in(key, 921), (2, TOKENS, KVH * HD), jnp.float32), -6.0, 6.0)
    return values.astype(jnp.bfloat16)


def draw_page_pool(key, part):
    host_count = REQS // REQ_HOST
    values = jnp.clip(jax.random.normal(jax.random.fold_in(key, 931), (host_count * SLOTS, 2, PAGE, KVH * HD), jnp.float32), -6.0, 6.0)
    return values.astype(jnp.bfloat16)


def split_up(count, total, limit, slope):
    loads = [(1 << 20) // math.isqrt(standing ** slope) + 1 for standing in range(2, count + 1)]
    surplus, holding = total - limit - (count - 1), [1] * (count - 1)
    while surplus > 0:
        candidates = [i for i in range(count - 1) if holding[i] < limit]
        mass, budget = sum([loads[i] for i in candidates]), surplus
        for i in candidates:
            addition = min(limit - holding[i], max(1, budget * loads[i] // mass), surplus)
            holding[i] = holding[i] + addition
            surplus = surplus - addition
    return np.array([limit] + holding)


def uneven(own_key, count, total, most, slope):
    if count == 2:
        one = jax.random.randint(own_key, (), max(1, total - most), min(most, total - 1) + 1)
        return jnp.stack([one, total - one])
    sizes = jnp.asarray(split_up(count, total, most, slope), jnp.int32)
    couples = (count - 1) // 2
    giver, taker = sizes[1:1 + 2 * couples:2], sizes[2:2 + 2 * couples:2]
    margin = jnp.minimum(giver - 1, most - taker)
    moved = jax.random.randint(jax.random.fold_in(own_key, 1), (couples,), 0, 1 << 20) % (margin + 1)
    sizes = sizes.at[1:1 + 2 * couples:2].set(giver - moved).at[2:2 + 2 * couples:2].set(taker + moved)
    return sizes[jax.random.permutation(jax.random.fold_in(own_key, 2), count)]


def setup_inputs(seed: int = 0) -> dict:
    seeds = jax.random.split(jax.random.key(seed), 8)
    queries = draw_queries(jax.random.fold_in(seeds[7], 71), 0)
    fresh_kv = draw_fresh_kv(jax.random.fold_in(seeds[7], 71), 0)
    page_pool = draw_page_pool(jax.random.fold_in(seeds[7], 71), 0)
    page_host = draw_page_host(jax.random.fold_in(seeds[7], 71), 0)
    page_slot = draw_page_slot(jax.random.fold_in(seeds[7], 71), 0)
    prefix_len = draw_prefix_len(jax.random.fold_in(seeds[7], 71), 0)
    fresh_len = jax.vmap(lambda own: uneven(own, REQ_HOST, TOK_HOST, MOST_NEW, 2))(jax.random.split(seeds[6], N_STORE)).reshape((N_STORE, REQ_HOST)).astype(jnp.int32)
    return {"queries": queries, "fresh_kv": fresh_kv, "page_pool": page_pool, "page_host": page_host, "page_slot": page_slot, "prefix_len": prefix_len, "fresh_len": fresh_len}


def request_attention(q_rows, key_rows, value_rows, key_valid):
    scores = jnp.einsum('mkgd,nkd->kgmn', q_rows.astype(jnp.float32), key_rows.astype(jnp.float32)) * (1.0 / math.sqrt(HD))
    row_top = lax.optimization_barrier(jnp.max(jnp.where(key_valid, scores, -1e+30), axis=-1, keepdims=True))
    weights = jnp.where(key_valid, jnp.exp(scores - row_top), 0.0)
    row_total = lax.optimization_barrier(jnp.sum(weights, axis=-1))
    rounded = lax.optimization_barrier(weights.astype(jnp.bfloat16))
    mixed_rows = jnp.einsum('kgmn,nkd->mkgd', rounded.astype(jnp.float32), value_rows.astype(jnp.float32))
    return (mixed_rows / jnp.transpose(row_total, (2, 0, 1))[..., None]).astype(jnp.bfloat16)

def reference(queries, fresh_kv, page_pool, page_host, page_slot, prefix_len, fresh_len):
    group_size = QH // KVH
    offsets = (jnp.cumsum(fresh_len, axis=1) - fresh_len).astype(jnp.int32)
    positions = jnp.arange(MOST_NEW, dtype=jnp.int32)
    cache_index = jnp.arange(PAGES_MAX * PAGE, dtype=jnp.int32)

    def one_request(request_id, output):
        request_id = jnp.asarray(request_id).astype(jnp.int32)
        host_id = (request_id // REQ_HOST).astype(jnp.int32)
        within = (request_id % REQ_HOST).astype(jnp.int32)
        offset = offsets[host_id, within].astype(jnp.int32)
        length = fresh_len[host_id, within].astype(jnp.int32)
        window_start = jnp.minimum(offset, TOK_HOST - MOST_NEW).astype(jnp.int32)
        first_row = (host_id * TOK_HOST + window_start).astype(jnp.int32)
        q_rows = lax.dynamic_slice_in_dim(queries, first_row, MOST_NEW, 0).reshape(MOST_NEW, KVH, group_size, HD)
        new_rows = lax.dynamic_slice_in_dim(fresh_kv, first_row, MOST_NEW, 1).reshape(2, MOST_NEW, KVH, HD)
        page_ids = (page_host[request_id] * SLOTS + page_slot[request_id]).astype(jnp.int32)
        cached = page_pool[page_ids]
        cached_keys = cached[:, 0].reshape(PAGES_MAX * PAGE, KVH, HD)
        cached_values = cached[:, 1].reshape(PAGES_MAX * PAGE, KVH, HD)
        key_rows = jnp.concatenate([cached_keys, new_rows[0]], axis=0)
        value_rows = jnp.concatenate([cached_values, new_rows[1]], axis=0)
        query_pos = window_start + positions
        cache_ok = jnp.broadcast_to(cache_index[None, :] < prefix_len[request_id], (MOST_NEW, PAGES_MAX * PAGE))
        fresh_ok = (query_pos[None, :] >= offset) & (query_pos[None, :] <= query_pos[:, None])
        key_valid = jnp.concatenate([cache_ok, fresh_ok], axis=1)
        mixed_rows = request_attention(q_rows, key_rows, value_rows, key_valid).reshape(MOST_NEW, QH * HD)
        row_ok = (query_pos >= offset) & (query_pos < offset + length)
        old_rows = lax.dynamic_slice_in_dim(output, first_row, MOST_NEW, 0)
        return lax.dynamic_update_slice_in_dim(output, jnp.where(row_ok[:, None], mixed_rows, old_rows), first_row, 0)
    return lax.fori_loop(0, REQS, one_request, jnp.zeros_like(queries))
```

```python
import functools
import math

import jax
import jax.numpy as jnp
from jax import lax
from jax.experimental import pallas as pl
from jax.experimental.pallas import tpu as pltpu
from jax.sharding import PartitionSpec as P

HD = 128
PAGE = 128
CAP = 2
NEG = -1e30
MESH = pl.DeviceIdType.MESH
LANES = 128


def exchange_kernel(
    stores, tps, codes_ref, fresh_ref, pool_ref, arrived_ref, new_ref,
    want, got, got_s, pool_v, send_v,
    local_sem, want_send, want_recv, page_send, page_recv, new_send, new_recv,
):
    me = lax.axis_index("store")
    mt = lax.axis_index("tp")
    slots = pool_v.shape[0]
    rows = fresh_ref.shape[1]

    pool_copy = pltpu.make_async_copy(pool_ref, pool_v, local_sem.at[0])
    pool_copy.start()
    own_new = pltpu.make_async_copy(
        fresh_ref.at[:, :, pl.ds(pl.multiple_of(mt * HD, HD), HD)],
        new_ref.at[:, pl.ds(pl.multiple_of(mt * rows, rows), rows), :],
        local_sem.at[1],
    )
    own_new.start()

    barrier = pltpu.get_barrier_semaphore()

    def greet_store(i, c):
        d = lax.rem(me + i, stores)
        pl.semaphore_signal(barrier, inc=1, device_id={"store": d}, device_id_type=MESH)
        return c

    def greet_tp(i, c):
        d = lax.rem(mt + i, tps)
        pl.semaphore_signal(barrier, inc=1, device_id={"tp": d}, device_id_type=MESH)
        return c

    lax.fori_loop(1, stores, greet_store, 0)
    lax.fori_loop(1, tps, greet_tp, 0)

    codes = codes_ref[0:1, :]
    owner = lax.shift_right_arithmetic(codes, 12)
    item = jnp.bitwise_and(codes, 4095)
    source = lax.broadcasted_iota(jnp.int32, (stores, LANES), 0)
    lane = lax.broadcasted_iota(jnp.int32, (stores, LANES), 1)
    match = jnp.broadcast_to(owner, (stores, LANES)) == source
    item = jnp.broadcast_to(item, (stores, LANES))
    first = jnp.min(jnp.where(match, item, 4095), axis=1, keepdims=True)
    second = jnp.max(jnp.where(match, item, 0), axis=1, keepdims=True)
    both = jnp.where(lane == 0, first, second)
    want[...] = jnp.bitwise_and(both, slots - 1).reshape(stores, 1, LANES)

    pl.semaphore_wait(barrier, stores - 1 + tps - 1)

    def new_copy(i):
        d = lax.rem(mt + i, tps)
        return pltpu.make_async_remote_copy(
            src_ref=fresh_ref.at[:, :, pl.ds(pl.multiple_of(d * HD, HD), HD)],
            dst_ref=new_ref.at[:, pl.ds(pl.multiple_of(mt * rows, rows), rows), :],
            send_sem=new_send.at[i],
            recv_sem=new_recv.at[i],
            device_id={"tp": d},
            device_id_type=MESH,
        )

    def want_copy(i):
        d = lax.rem(me + i, stores)
        return pltpu.make_async_remote_copy(
            src_ref=want.at[d],
            dst_ref=got.at[me],
            send_sem=want_send.at[i],
            recv_sem=want_recv.at[i],
            device_id={"store": d},
            device_id_type=MESH,
        )

    def page_copy(i):
        d = lax.rem(me + i, stores)
        return pltpu.make_async_remote_copy(
            src_ref=send_v.at[d],
            dst_ref=arrived_ref.at[me],
            send_sem=page_send.at[i],
            recv_sem=page_recv.at[i],
            device_id={"store": d},
            device_id_type=MESH,
        )

    def run(start, stop, body):
        def step(i, c):
            body(i)
            return c
        lax.fori_loop(start, stop, step, 0)

    run(1, stores, lambda i: want_copy(i).start())
    run(1, tps, lambda i: new_copy(i).start())
    got_own = pltpu.make_async_copy(want.at[me], got.at[me], local_sem.at[2])
    got_own.start()
    got_own.wait()
    run(1, stores, lambda i: want_copy(i).wait())
    scalars = pltpu.make_async_copy(got, got_s, local_sem.at[3])
    scalars.start()
    pool_copy.wait()
    scalars.wait()

    def pack(i):
        d = lax.rem(me + i, stores)
        send_v[d, 0] = pool_v[got_s[d, 0, 0]]
        send_v[d, 1] = pool_v[got_s[d, 0, 1]]

    def pack_send(i):
        pack(i)
        page_copy(i).start()

    run(1, stores, pack_send)
    pack(0)
    own = pltpu.make_async_copy(send_v.at[me], arrived_ref.at[me], local_sem.at[4])
    own.start()
    own.wait()
    own_new.wait()
    run(1, tps, lambda i: new_copy(i).wait())
    run(1, stores, lambda i: page_copy(i).wait())


def exchange(codes, fresh_kv, page_pool, stores, tps):
    slots, _, page, width = page_pool.shape
    rows = fresh_kv.shape[1]
    dt = page_pool.dtype
    any_spec = pl.BlockSpec(memory_space=pl.ANY)
    return pl.pallas_call(
        functools.partial(exchange_kernel, stores, tps),
        out_shape=(
            jax.ShapeDtypeStruct((stores, CAP, 2, page, width), dt),
            jax.ShapeDtypeStruct((2, rows * tps, HD), dt),
        ),
        in_specs=[pl.BlockSpec(memory_space=pltpu.VMEM), any_spec, any_spec],
        out_specs=(any_spec, any_spec),
        scratch_shapes=[
            pltpu.VMEM((stores, 1, LANES), jnp.int32),
            pltpu.VMEM((stores, 1, LANES), jnp.int32),
            pltpu.SMEM((stores, 1, LANES), jnp.int32),
            pltpu.VMEM((slots, 2, page, width), dt),
            pltpu.VMEM((stores, CAP, 2, page, width), dt),
            pltpu.SemaphoreType.DMA((5,)),
            pltpu.SemaphoreType.DMA((stores,)),
            pltpu.SemaphoreType.DMA((stores,)),
            pltpu.SemaphoreType.DMA((stores,)),
            pltpu.SemaphoreType.DMA((stores,)),
            pltpu.SemaphoreType.DMA((tps,)),
            pltpu.SemaphoreType.DMA((tps,)),
        ],
        compiler_params=pltpu.CompilerParams(
            collective_id=0, has_side_effects=True, vmem_limit_bytes=24 << 20
        ),
        name="exchange",
    )(codes, fresh_kv, page_pool)


ROWS = 64
KEYS = 256


def attend_kernel(
    heads, host_s, slot_s, prefix_s, length_s, q_ref, new_ref, arrived_ref, out_ref,
    kv, fresh, scores, top, acc, count, page_sem, new_sem,
):
    requests, pages = host_s.shape
    stores = count.shape[0]
    block_rows = q_ref.shape[0]
    scale = math.log2(math.e) / math.sqrt(HD)
    stack = ROWS * heads

    new_copy = pltpu.make_async_copy(new_ref, fresh, new_sem)
    new_copy.start()

    def clear(i, c):
        count[i] = 0
        return c

    lax.fori_loop(0, stores, clear, 0)

    def page_copies(r, p, at):
        return [
            pltpu.make_async_copy(
                arrived_ref.at[at, half],
                kv.at[r, half, pl.ds(pl.multiple_of(p * PAGE, PAGE), PAGE), :],
                page_sem.at[r, p, half],
            )
            for half in range(2)
        ]

    for r in range(requests):
        used = lax.div(prefix_s[r] + (PAGE - 1), PAGE)

        def fetch(p, last):
            host = host_s[r, p]
            rank = count[host]
            count[host] = jnp.where(p < used, rank + 1, rank)
            at = jnp.where(p < used, host * CAP + jnp.minimum(rank, CAP - 1), last)
            for copy in page_copies(r, p, at):
                copy.start()
            return at

        lax.fori_loop(0, pages, fetch, 0)

    new_copy.wait()
    key_lane = lax.broadcasted_iota(jnp.int32, (stack, KEYS), 1)
    row_in_block = lax.rem(lax.broadcasted_iota(jnp.int32, (stack, KEYS), 0), ROWS)
    ones = jnp.ones((KEYS, HD), jnp.bfloat16)
    out_row = lax.broadcasted_iota(jnp.int32, (ROWS, HD), 0)

    def one_request(r, offset):
        length = length_s[0, r]
        prefix = prefix_s[r]

        def wait_page(p, c):
            for copy in page_copies(r, p, 0):
                copy.wait()
            return c

        lax.fori_loop(0, pages, wait_page, 0)
        chunks = lax.div(prefix + (KEYS - 1), KEYS)

        def one_block(b, c):
            row0 = pl.multiple_of(b * ROWS, ROWS)
            q = q_ref[pl.ds(row0, ROWS), :]
            q = jnp.concatenate([q[:, h * HD:(h + 1) * HD] for h in range(heads)], axis=0)
            top[...] = jnp.full((stack, HD), NEG, jnp.float32)

            def note(s, at):
                scores[at] = s
                top[...] = jnp.maximum(top[...], jnp.maximum(s[:, :HD], s[:, HD:]))

            def dot(k):
                return lax.dot_general(
                    q, k, (((1,), (1,)), ((), ())), preferred_element_type=jnp.float32
                )

            def cached(i, c):
                note(dot(kv[r, 0, pl.ds(pl.multiple_of(i * KEYS, KEYS), KEYS), :]), i)
                return c

            lax.fori_loop(0, chunks - 1, cached, 0)
            last = chunks - 1
            s = dot(kv[r, 0, pl.ds(pl.multiple_of(last * KEYS, KEYS), KEYS), :])
            note(jnp.where(key_lane < prefix - last * KEYS, s, NEG), last)

            f0 = lax.div(offset, KEYS)
            f1 = lax.div(row0 + (ROWS - 1), KEYS) + 1

            def new_keys(i, c):
                s = dot(fresh[0, pl.ds(pl.multiple_of(i * KEYS, KEYS), KEYS), :])
                key = key_lane + i * KEYS
                ok = (key >= offset) & (key <= row_in_block + row0)
                note(jnp.where(ok, s, NEG), chunks + i - f0)
                return c

            lax.fori_loop(f0, f1, new_keys, 0)
            m = jnp.max(top[...], axis=1, keepdims=True) * scale
            acc[...] = jnp.zeros((stack, 2 * HD), jnp.float32)

            def mix(at, v):
                w = jnp.exp2(scores[at] * scale - m).astype(jnp.bfloat16)
                v = jnp.concatenate([v, ones], axis=1)
                acc[...] += jnp.dot(w, v, preferred_element_type=jnp.float32)

            def cached_mix(i, c):
                mix(i, kv[r, 1, pl.ds(pl.multiple_of(i * KEYS, KEYS), KEYS), :])
                return c

            lax.fori_loop(0, chunks, cached_mix, 0)

            def new_mix(i, c):
                mix(chunks + i - f0, fresh[1, pl.ds(pl.multiple_of(i * KEYS, KEYS), KEYS), :])
                return c

            lax.fori_loop(f0, f1, new_mix, 0)
            mine = (out_row + row0 >= offset) & (out_row + row0 < offset + length)
            for h in range(heads):
                a = acc[h * ROWS:(h + 1) * ROWS, :]
                o = (a[:, :HD] / a[:, HD:]).astype(jnp.bfloat16)
                old = out_ref[pl.ds(row0, ROWS), h * HD:(h + 1) * HD]
                out_ref[pl.ds(row0, ROWS), h * HD:(h + 1) * HD] = jnp.where(mine, o, old)
            return c

        lax.fori_loop(lax.div(offset, ROWS), lax.div(offset + length - 1, ROWS) + 1, one_block, 0)
        return offset + length

    lax.fori_loop(0, requests, one_request, 0)


def attention(queries, new_kv, arrived, page_host, page_slot, prefix_len, fresh_len):
    block_rows, width = queries.shape
    requests, pages = page_host.shape
    heads = width // HD
    stores = arrived.shape[0]
    stack = ROWS * heads
    keys = pages * PAGE
    smem = pl.BlockSpec(memory_space=pltpu.SMEM)
    any_spec = pl.BlockSpec(memory_space=pl.ANY)
    vmem = pl.BlockSpec(memory_space=pltpu.VMEM)
    flat = arrived.reshape(stores * CAP, 2, PAGE, HD)
    return pl.pallas_call(
        functools.partial(attend_kernel, heads),
        out_shape=jax.ShapeDtypeStruct((block_rows, width), queries.dtype),
        in_specs=[smem, smem, smem, smem, vmem, any_spec, any_spec],
        out_specs=vmem,
        scratch_shapes=[
            pltpu.VMEM((requests, 2, keys, HD), jnp.bfloat16),
            pltpu.VMEM((2, block_rows, HD), jnp.bfloat16),
            pltpu.VMEM(((keys + 2 * KEYS + KEYS) // KEYS, stack, KEYS), jnp.float32),
            pltpu.VMEM((stack, HD), jnp.float32),
            pltpu.VMEM((stack, 2 * HD), jnp.float32),
            pltpu.SMEM((stores,), jnp.int32),
            pltpu.SemaphoreType.DMA((requests, pages, 2)),
            pltpu.SemaphoreType.DMA,
        ],
        compiler_params=pltpu.CompilerParams(vmem_limit_bytes=40 << 20),
        name="attend",
    )(page_host, page_slot, prefix_len, fresh_len, queries, new_kv, flat)


def local(queries, fresh_kv, page_pool, page_host, page_slot, prefix_len, fresh_len):
    stores = lax.axis_size("store")
    tps = lax.axis_size("tp")
    requests, pages = page_host.shape
    entries = requests * pages
    page = lax.broadcasted_iota(jnp.int32, (requests, pages), 1)
    entry = lax.broadcasted_iota(jnp.int32, (requests, pages), 0) * pages + page
    in_use = page * PAGE < prefix_len[:, None]
    codes = jnp.where(in_use, page_host, stores) * 4096 + entry * 64 + page_slot
    codes = codes.reshape(1, entries)
    codes = jnp.pad(codes, ((0, 0), (0, LANES - entries)), constant_values=stores * 4096)
    codes = jnp.broadcast_to(codes, (8, LANES))
    arrived, new_kv = exchange(codes, fresh_kv, page_pool, stores, tps)
    return attention(queries, new_kv, arrived, page_host, page_slot, prefix_len, fresh_len)


def solution(mesh):
    placed = (
        P("store", "tp"),
        P(None, ("store", "tp"), None),
        P("store", None, None, "tp"),
        P("store", None),
        P("store", None),
        P("store"),
        P("store", None),
    )
    return jax.shard_map(
        local, mesh=mesh, in_specs=placed, out_specs=P("store", "tp"), check_vma=False
    )
```

```python
import functools
import math

import jax
import jax.numpy as jnp
from jax import lax
from jax.experimental import pallas as pl
from jax.experimental.pallas import tpu as pltpu
from jax.sharding import PartitionSpec as P

HD = 128
PAGE = 128
CAP = 2
NEG = -1e30
MESH = pl.DeviceIdType.MESH
LANES = 128


def exchange_kernel(
    stores, tps, codes_ref, fresh_ref, pool_ref, arrived_ref, new_ref,
    want, got, got_s, pool_v, send_v,
    local_sem, want_send, want_recv, page_send, page_recv, new_send, new_recv,
):
    me = lax.axis_index("store")
    mt = lax.axis_index("tp")
    slots = pool_v.shape[0]

    pool_copy = pltpu.make_async_copy(pool_ref, pool_v, local_sem.at[0])
    pool_copy.start()
    own_new = pltpu.make_async_copy(
        fresh_ref.at[:, :, pl.ds(pl.multiple_of(mt * HD, HD), HD)],
        new_ref.at[mt],
        local_sem.at[1],
    )
    own_new.start()

    barrier = pltpu.get_barrier_semaphore()

    def greet_store(i, c):
        d = lax.rem(me + i, stores)
        pl.semaphore_signal(barrier, inc=1, device_id={"store": d}, device_id_type=MESH)
        return c

    def greet_tp(i, c):
        d = lax.rem(mt + i, tps)
        pl.semaphore_signal(barrier, inc=1, device_id={"tp": d}, device_id_type=MESH)
        return c

    lax.fori_loop(1, stores, greet_store, 0)
    lax.fori_loop(1, tps, greet_tp, 0)

    codes = codes_ref[0:1, :]
    owner = lax.shift_right_arithmetic(codes, 12)
    item = jnp.bitwise_and(codes, 4095)
    source = lax.broadcasted_iota(jnp.int32, (stores, LANES), 0)
    lane = lax.broadcasted_iota(jnp.int32, (stores, LANES), 1)
    match = jnp.broadcast_to(owner, (stores, LANES)) == source
    item = jnp.broadcast_to(item, (stores, LANES))
    first = jnp.min(jnp.where(match, item, 4095), axis=1, keepdims=True)
    second = jnp.max(jnp.where(match, item, 0), axis=1, keepdims=True)
    both = jnp.where(lane == 0, first, second)
    want[...] = jnp.bitwise_and(both, slots - 1).reshape(stores, 1, LANES)

    pl.semaphore_wait(barrier, stores - 1 + tps - 1)

    def new_copy(i):
        d = lax.rem(mt + i, tps)
        return pltpu.make_async_remote_copy(
            src_ref=fresh_ref.at[:, :, pl.ds(pl.multiple_of(d * HD, HD), HD)],
            dst_ref=new_ref.at[mt],
            send_sem=new_send.at[i],
            recv_sem=new_recv.at[i],
            device_id={"tp": d},
            device_id_type=MESH,
        )

    def want_copy(i):
        d = lax.rem(me + i, stores)
        return pltpu.make_async_remote_copy(
            src_ref=want.at[d],
            dst_ref=got.at[me],
            send_sem=want_send.at[i],
            recv_sem=want_recv.at[i],
            device_id={"store": d},
            device_id_type=MESH,
        )

    def page_copy(i):
        d = lax.rem(me + i, stores)
        return pltpu.make_async_remote_copy(
            src_ref=send_v.at[d],
            dst_ref=arrived_ref.at[me],
            send_sem=page_send.at[i],
            recv_sem=page_recv.at[i],
            device_id={"store": d},
            device_id_type=MESH,
        )

    def run(start, stop, body):
        def step(i, c):
            body(i)
            return c
        lax.fori_loop(start, stop, step, 0)

    run(1, stores, lambda i: want_copy(i).start())
    run(1, tps, lambda i: new_copy(i).start())
    got_own = pltpu.make_async_copy(want.at[me], got.at[me], local_sem.at[2])
    got_own.start()
    got_own.wait()
    run(1, stores, lambda i: want_copy(i).wait())
    scalars = pltpu.make_async_copy(got, got_s, local_sem.at[3])
    scalars.start()
    pool_copy.wait()
    scalars.wait()

    def pack(i):
        d = lax.rem(me + i, stores)
        send_v[d, 0] = pool_v[got_s[d, 0, 0]]
        send_v[d, 1] = pool_v[got_s[d, 0, 1]]

    def pack_send(i):
        pack(i)
        page_copy(i).start()

    run(1, stores, pack_send)
    pack(0)
    own = pltpu.make_async_copy(send_v.at[me], arrived_ref.at[me], local_sem.at[4])
    own.start()
    own.wait()
    own_new.wait()
    run(1, tps, lambda i: new_copy(i).wait())
    run(1, stores, lambda i: page_copy(i).wait())


def exchange(codes, fresh_kv, page_pool, stores, tps):
    slots, _, page, width = page_pool.shape
    rows = fresh_kv.shape[1]
    dt = page_pool.dtype
    any_spec = pl.BlockSpec(memory_space=pl.ANY)
    hbm_spec = pl.BlockSpec(memory_space=pltpu.HBM)
    return pl.pallas_call(
        functools.partial(exchange_kernel, stores, tps),
        out_shape=(
            jax.ShapeDtypeStruct((stores, CAP, 2, page, width), dt),
            jax.ShapeDtypeStruct((tps, 2, rows, HD), dt),
        ),
        in_specs=[pl.BlockSpec(memory_space=pltpu.VMEM), hbm_spec, hbm_spec],
        out_specs=(any_spec, any_spec),
        scratch_shapes=[
            pltpu.VMEM((stores, 1, LANES), jnp.int32),
            pltpu.VMEM((stores, 1, LANES), jnp.int32),
            pltpu.SMEM((stores, 1, LANES), jnp.int32),
            pltpu.VMEM((slots, 2, page, width), dt),
            pltpu.VMEM((stores, CAP, 2, page, width), dt),
            pltpu.SemaphoreType.DMA((5,)),
            pltpu.SemaphoreType.DMA((stores,)),
            pltpu.SemaphoreType.DMA((stores,)),
            pltpu.SemaphoreType.DMA((stores,)),
            pltpu.SemaphoreType.DMA((stores,)),
            pltpu.SemaphoreType.DMA((tps,)),
            pltpu.SemaphoreType.DMA((tps,)),
        ],
        compiler_params=pltpu.CompilerParams(
            collective_id=0, has_side_effects=True, vmem_limit_bytes=24 << 20
        ),
        name="exchange",
    )(codes, fresh_kv, page_pool)


ROWS = 64
KEYS = 256
FAR = 1 << 20


def attend_kernel(
    heads, host_s, prefix_s, length_s, q_ref, new_ref, arrived_ref, out_ref,
    kv, row_id, scores, count, page_sem, new_sem,
):
    requests, pages = host_s.shape
    stores = count.shape[0]
    blocks = new_ref.shape[0]
    cached_pages = requests * pages
    scale = math.log2(math.e) / math.sqrt(HD)
    stack = ROWS * heads

    new_copy = pltpu.make_async_copy(new_ref, kv.at[pl.ds(cached_pages, blocks)], new_sem)
    new_copy.start()

    def clear(i, c):
        count[i] = 0
        return c

    lax.fori_loop(0, stores, clear, 0)

    def page_copy(r, p, at):
        return pltpu.make_async_copy(
            arrived_ref.at[at], kv.at[r * pages + p], page_sem.at[r, p]
        )

    def used_pages(r):
        return lax.div(prefix_s[r] + (PAGE - 1), PAGE)

    for r in range(requests):
        def fetch(p, c):
            host = host_s[r, p]
            rank = count[host]
            count[host] = rank + 1
            page_copy(r, p, host * CAP + jnp.minimum(rank, CAP - 1)).start()
            return c

        lax.fori_loop(0, used_pages(r), fetch, 0)

    row_id[...] = (
        lax.broadcasted_iota(jnp.int32, (stack, HD), 1)
        == lax.rem(lax.broadcasted_iota(jnp.int32, (stack, HD), 0), ROWS)
    ).astype(jnp.bfloat16)
    key_row = lax.broadcasted_iota(jnp.int32, (PAGE, HD), 0)
    key_lane = lax.broadcasted_iota(jnp.int32, (PAGE, HD), 1)
    ones = jnp.ones((PAGE, HD), jnp.bfloat16)
    no_mask = jnp.zeros((PAGE, HD), jnp.bfloat16)
    out_row = lax.broadcasted_iota(jnp.int32, (ROWS, HD), 0)
    new_copy.wait()

    def one_request(r, offset):
        length = length_s[0, r]
        prefix = prefix_s[r]
        used = used_pages(r)
        full = lax.div(prefix, PAGE)

        def wait_page(p, c):
            page_copy(r, p, 0).wait()
            return c

        lax.fori_loop(0, used, wait_page, 0)

        def one_block(b, c):
            row0 = pl.multiple_of(b * ROWS, ROWS)
            f0 = lax.div(offset, PAGE)
            f1 = lax.div(row0 + (ROWS - 1), PAGE) + 1
            total = used + f1 - f0

            def place(i):
                cached = i < used
                return jnp.where(
                    cached, r * pages + i, cached_pages + jnp.minimum(f0 + i - used, f1 - 1)
                )

            def mask(i):
                if i < 4:
                    return no_mask
                cached = i < used
                base = PAGE * (f0 + i - used)
                low = jnp.where(cached, 0, jnp.where(i < total, offset - base, FAR))
                high = jnp.where(cached, prefix - 1 - PAGE * i, row0 - base)
                slope = jnp.where(cached, 0, 1)
                ok = (key_row >= low) & (key_row <= high + key_lane * slope)
                return jnp.where(ok, 0.0, NEG).astype(jnp.bfloat16)

            q = q_ref[pl.ds(row0, ROWS), :]
            q = jnp.concatenate([q[:, h * HD:(h + 1) * HD] for h in range(heads)], axis=0)
            q = jnp.concatenate([q, row_id[...]], axis=1)
            mine = (out_row + row0 >= offset) & (out_row + row0 < offset + length)

            def variant(chunks):
                def body():
                    for j in range(chunks):
                        k = jnp.concatenate(
                            [
                                jnp.concatenate([kv[place(i), 0], mask(i)], axis=1)
                                for i in (2 * j, 2 * j + 1)
                            ],
                            axis=0,
                        )
                        scores[j] = lax.dot_general(
                            q, k, (((1,), (1,)), ((), ())), preferred_element_type=jnp.float32
                        )
                    top = scores[0]
                    for j in range(1, chunks):
                        top = jnp.maximum(top, scores[j])
                    top = jnp.max(top, axis=1, keepdims=True) * scale
                    mixed = None
                    for j in range(chunks):
                        w = jnp.exp2(scores[j] * scale - top).astype(jnp.bfloat16)
                        v = jnp.concatenate(
                            [
                                jnp.concatenate([kv[place(i), 1], ones], axis=1)
                                for i in (2 * j, 2 * j + 1)
                            ],
                            axis=0,
                        )
                        part = jnp.dot(w, v, preferred_element_type=jnp.float32)
                        mixed = part if mixed is None else mixed + part
                    result = (mixed[:, :HD] / mixed[:, HD:]).astype(jnp.bfloat16)
                    for h in range(heads):
                        at = (pl.ds(row0, ROWS), slice(h * HD, (h + 1) * HD))
                        out_ref[at] = jnp.where(
                            mine, result[h * ROWS:(h + 1) * ROWS], out_ref[at]
                        )
                return body

            chunks = lax.div(total + 1, 2)
            for n in range(3, 7):
                pl.when(chunks == n)(variant(n))
            return c

        lax.fori_loop(lax.div(offset, ROWS), lax.div(offset + length - 1, ROWS) + 1, one_block, 0)
        return offset + length

    lax.fori_loop(0, requests, one_request, 0)


def attention(queries, new_kv, arrived, page_host, prefix_len, fresh_len):
    block_rows, width = queries.shape
    requests, pages = page_host.shape
    heads = width // HD
    stores = arrived.shape[0]
    stack = ROWS * heads
    smem = pl.BlockSpec(memory_space=pltpu.SMEM)
    any_spec = pl.BlockSpec(memory_space=pl.ANY)
    vmem = pl.BlockSpec(memory_space=pltpu.VMEM)
    flat = arrived.reshape(stores * CAP, 2, PAGE, HD)
    return pl.pallas_call(
        functools.partial(attend_kernel, heads),
        out_shape=jax.ShapeDtypeStruct((block_rows, width), queries.dtype),
        in_specs=[smem, smem, smem, vmem, any_spec, any_spec],
        out_specs=vmem,
        scratch_shapes=[
            pltpu.VMEM((requests * pages + new_kv.shape[0], 2, PAGE, HD), jnp.bfloat16),
            pltpu.VMEM((stack, HD), jnp.bfloat16),
            pltpu.VMEM((6, stack, KEYS), jnp.float32),
            pltpu.SMEM((stores,), jnp.int32),
            pltpu.SemaphoreType.DMA((requests, pages)),
            pltpu.SemaphoreType.DMA,
        ],
        compiler_params=pltpu.CompilerParams(vmem_limit_bytes=40 << 20),
        name="attend",
    )(page_host, prefix_len, fresh_len, queries, new_kv, flat)


def local(queries, fresh_kv, page_pool, page_host, page_slot, prefix_len, fresh_len):
    stores = lax.axis_size("store")
    tps = lax.axis_size("tp")
    requests, pages = page_host.shape
    entries = requests * pages
    page = lax.broadcasted_iota(jnp.int32, (requests, pages), 1)
    entry = lax.broadcasted_iota(jnp.int32, (requests, pages), 0) * pages + page
    in_use = page * PAGE < prefix_len[:, None]
    codes = jnp.where(in_use, page_host, stores) * 4096 + entry * 64 + page_slot
    codes = codes.reshape(1, entries)
    codes = jnp.pad(codes, ((0, 0), (0, LANES - entries)), constant_values=stores * 4096)
    codes = jnp.broadcast_to(codes, (8, LANES))
    arrived, new_kv = exchange(codes, fresh_kv, page_pool, stores, tps)
    return attention(queries, new_kv, arrived, page_host, prefix_len, fresh_len)


def solution(mesh):
    placed = (
        P("store", "tp"),
        P(None, ("store", "tp"), None),
        P("store", None, None, "tp"),
        P("store", None),
        P("store", None),
        P("store"),
        P("store", None),
    )
    return jax.shard_map(
        local, mesh=mesh, in_specs=placed, out_specs=P("store", "tp"), check_vma=False
    )
```

```python
import functools
import math

import jax
import jax.numpy as jnp
from jax import lax
from jax.experimental import pallas as pl
from jax.experimental.pallas import tpu as pltpu
from jax.sharding import PartitionSpec as P

HD = 128
PAGE = 128
LANES = 128
NEG = -1e30
FAR = 1 << 20
MESH = pl.DeviceIdType.MESH
RING = 8
ROWS = 64
EARLY = 10
SCALE = math.log2(math.e) / math.sqrt(HD)


def plan_kernel(host_s, slot_s, prefix_s, want_ref, plan_s, want_s, count, sem):
    requests, pages = host_s.shape
    stores = count.shape[0]
    entries = requests * pages

    def clear(i, c):
        count[i] = 0
        want_s[i, 0, 0] = 0
        want_s[i, 0, 1] = 0
        return c

    lax.fori_loop(0, stores, clear, 0)
    for r in range(requests):
        prefix = prefix_s[r]

        def one(p, c):
            n0, n1 = c
            host = host_s[r, p]
            rank = jnp.minimum(count[host], 1)
            count[host] = rank + 1
            want_s[host, 0, rank] = slot_s[r, p]
            at = rank * entries + r * pages + jnp.where(rank == 0, n0, n1)
            plan_s[at] = host * 256 + jnp.minimum(prefix - p * PAGE, PAGE)
            return n0 + 1 - rank, n1 + rank

        n0, n1 = lax.fori_loop(0, lax.div(prefix + (PAGE - 1), PAGE), one, (0, 0))
        plan_s[2 * entries + r] = n0
        plan_s[2 * entries + requests + r] = n1
    copy = pltpu.make_async_copy(want_s, want_ref, sem)
    copy.start()
    copy.wait()


def make_plan(page_host, page_slot, prefix_len, stores):
    requests, pages = page_host.shape
    smem = pl.BlockSpec(memory_space=pltpu.SMEM)
    return pl.pallas_call(
        plan_kernel,
        out_shape=(
            jax.ShapeDtypeStruct((stores, 1, LANES), jnp.int32),
            jax.ShapeDtypeStruct((2 * requests * pages + 2 * requests,), jnp.int32),
        ),
        in_specs=[smem, smem, smem],
        out_specs=(pl.BlockSpec(memory_space=pl.ANY), smem),
        scratch_shapes=[
            pltpu.SMEM((stores, 1, LANES), jnp.int32),
            pltpu.SMEM((stores,), jnp.int32),
            pltpu.SemaphoreType.DMA,
        ],
        name="plan",
    )(page_host, page_slot, prefix_len)


def one_hot_rows(stack):
    lane = lax.broadcasted_iota(jnp.int32, (stack, HD), 1)
    row = lax.rem(lax.broadcasted_iota(jnp.int32, (stack, HD), 0), ROWS)
    return (lane == row).astype(jnp.bfloat16)


def stacked(q, row_id, heads):
    q = jnp.concatenate([q[:, h * HD:(h + 1) * HD] for h in range(heads)], axis=0)
    return jnp.concatenate([q, row_id], axis=1)


def page_mask(low, high, slope):
    key = lax.broadcasted_iota(jnp.int32, (PAGE, HD), 0)
    lane = lax.broadcasted_iota(jnp.int32, (PAGE, HD), 1)
    ok = (key >= low) & (key <= high + lane * slope)
    return jnp.where(ok, 0.0, NEG).astype(jnp.bfloat16)


def attend_pages(q, keys, values, scores, top):
    chunks = len(keys) // 2
    ones = jnp.ones((PAGE, HD), jnp.bfloat16)
    for j in range(chunks):
        k = jnp.concatenate(
            [jnp.concatenate(keys[i](), axis=1) for i in (2 * j, 2 * j + 1)], axis=0
        )
        scores[j] = lax.dot_general(
            q, k, (((1,), (1,)), ((), ())), preferred_element_type=jnp.float32
        )
    best = scores[0]
    for j in range(1, chunks):
        best = jnp.maximum(best, scores[j])
    best = jnp.max(best, axis=1, keepdims=True) * SCALE
    top = best if top is None else jnp.maximum(top, best)
    mixed = None
    for j in range(chunks):
        w = jnp.exp2(scores[j] * SCALE - top).astype(jnp.bfloat16)
        v = jnp.concatenate(
            [jnp.concatenate([values[i](), ones], axis=1) for i in (2 * j, 2 * j + 1)], axis=0
        )
        part = jnp.dot(w, v, preferred_element_type=jnp.float32)
        mixed = part if mixed is None else mixed + part
    return top, mixed


def exchange_kernel(
    stores, tps, heads, plan_s, length_s, want, fresh_ref, pool_ref, q_ref,
    pages_ref, late_ref, state_ref,
    got, got_s, pool_v, send_v, q_v, row_id, scores, state,
    local_sem, state_sem, q_sem, want_send, want_recv, page_send, page_recv, new_send, new_recv,
):
    me = lax.axis_index("store")
    mt = lax.axis_index("tp")
    my_y, my_z = me // RING, me % RING
    requests = length_s.shape[1]
    items = state_ref.shape[0]
    stack = ROWS * heads
    entries = (plan_s.shape[0] - 2 * requests) // 2
    pages = entries // requests

    def local_copy(src, dst, n):
        return pltpu.make_async_copy(src, dst, local_sem.at[n])

    pool_copy = local_copy(pool_ref, pool_v, 0)
    pool_copy.start()
    own_new = local_copy(
        fresh_ref.at[:, :, pl.ds(pl.multiple_of(mt * HD, HD), HD)], pages_ref.at[stores + mt], 1
    )
    own_new.start()
    blocks = q_v.shape[0]

    def q_copy(i):
        return pltpu.make_async_copy(
            q_ref.at[pl.ds(pl.multiple_of(i * ROWS, ROWS), ROWS), :], q_v.at[i], q_sem.at[i]
        )


    def run(start, stop, body):
        def step(i, c):
            body(i)
            return c
        lax.fori_loop(start, stop, step, 0)

    def partner(i):
        turn = i // (stores // RING)
        half = (turn + 1) // 2
        odd = turn % 2
        dz = odd * half + (1 - odd) * (RING - half)
        dy = i % (stores // RING)
        return ((my_y + dy) % (stores // RING)) * RING + (my_z + dz) % RING

    run(0, blocks, lambda i: q_copy(i).start())
    barrier = pltpu.get_barrier_semaphore()

    def greet(axis, d):
        pl.semaphore_signal(barrier, inc=1, device_id={axis: d}, device_id_type=MESH)

    run(1, stores, lambda i: greet("store", partner(i)))
    run(1, tps, lambda i: greet("tp", (mt + i) % tps))
    pl.semaphore_wait(barrier, stores - 1 + tps - 1)

    def remote(src, dst, send, recv, axis, d):
        return pltpu.make_async_remote_copy(
            src_ref=src, dst_ref=dst, send_sem=send, recv_sem=recv,
            device_id={axis: d}, device_id_type=MESH,
        )

    def new_copy(i):
        d = (mt + i) % tps
        return remote(
            fresh_ref.at[:, :, pl.ds(pl.multiple_of(d * HD, HD), HD)],
            pages_ref.at[stores + mt], new_send.at[i], new_recv.at[i], "tp", d,
        )

    def want_copy(i):
        d = partner(i)
        return remote(want.at[d], got.at[me], want_send.at[i], want_recv.at[i], "store", d)

    def page_copy(k, i):
        d = partner(i)
        dst = pages_ref.at[me] if k == 0 else late_ref.at[me]
        return remote(
            send_v.at[k, d], dst, page_send.at[k, i], page_recv.at[k, i], "store", d
        )

    run(1, stores, lambda i: want_copy(i).start())
    run(1, tps, lambda i: new_copy(i).start())
    got_own = local_copy(want.at[me], got.at[me], 3)
    got_own.start()
    row_id[...] = one_hot_rows(stack)
    got_own.wait()
    run(1, stores, lambda i: want_copy(i).wait())
    scalars = local_copy(got, got_s, 4)
    scalars.start()
    pool_copy.wait()
    scalars.wait()

    for k in range(2):
        def pack(i):
            d = partner(i)
            send_v[k, d] = pool_v[got_s[d, 0, k]]
            page_copy(k, i).start()
        run(1, stores, pack)
        send_v[k, me] = pool_v[got_s[me, 0, k]]
    own = [
        local_copy(send_v.at[0, me], pages_ref.at[me], 5),
        local_copy(send_v.at[1, me], late_ref.at[me], 6),
    ]
    for copy in own:
        copy.start()
    for copy in own:
        copy.wait()
    own_new.wait()
    run(0, blocks, lambda i: q_copy(i).wait())
    run(1, tps, lambda i: new_copy(i).wait())
    run(1, stores, lambda i: page_copy(0, i).wait())

    lane = lax.broadcasted_iota(jnp.int32, (stack, HD), 1)

    def one_item(item, c):
        r, row0, offset = find_item(length_s, item)
        f0 = offset // PAGE
        new = (row0 + (ROWS - 1)) // PAGE + 1 - f0
        early = new + plan_s[2 * entries + r]

        def entry(i):
            is_new = i < new
            j = jnp.clip(i - new, 0, pages - 1)
            code = plan_s[r * pages + j]
            base = PAGE * (f0 + i)
            used = i < early
            place = jnp.where(is_new, stores + f0 + i, jnp.where(used, code // 256, 0))
            place = jnp.clip(place, 0, stores + tps - 1)
            low = jnp.where(is_new, offset - base, jnp.where(used, 0, FAR))
            high = jnp.where(is_new, row0 - base, code % 256 - 1)
            return place, page_mask(low, high, jnp.where(is_new, 1, 0))

        def key(i):
            place, mask = entry(i)
            return [pages_ref[place, 0], mask]

        def value(i):
            place, _ = entry(i)
            return pages_ref[place, 1]

        q = stacked(q_v[jnp.clip(row0 // ROWS, 0, blocks - 1)], row_id[...], heads)
        top, mixed = attend_pages(
            q,
            [functools.partial(key, i) for i in range(EARLY)],
            [functools.partial(value, i) for i in range(EARLY)],
            scores, None,
        )
        slot = item % 2

        @pl.when(item >= 2)
        def _():
            state_copy(item - 2).wait()

        state[slot, :, :HD] = mixed[:, :HD]
        state[slot, :, HD:] = jnp.where(lane < HD // 2, mixed[:, HD:], top)
        state_copy(item).start()
        return c

    def state_copy(item):
        slot = item % 2
        return pltpu.make_async_copy(state.at[slot], state_ref.at[item], state_sem.at[slot])

    lax.fori_loop(0, items, one_item, 0)
    state_copy(items - 2).wait()
    state_copy(items - 1).wait()
    run(1, stores, lambda i: page_copy(1, i).wait())


def find_item(length_s, item):
    requests = length_s.shape[1]
    offset = 0
    start = 0
    r = 0
    row0 = 0
    at = 0
    for q in range(requests):
        length = length_s[0, q]
        first = offset // ROWS
        count = (offset + length - 1) // ROWS - first + 1
        here = item >= start
        block = jnp.maximum(first + jnp.minimum(item - start, count - 1), 0)
        r = jnp.where(here, q, r)
        row0 = jnp.where(here, block * ROWS, row0)
        at = jnp.where(here, offset, at)
        start = start + count
        offset = offset + length
    return r, row0, at


def exchange(plan, want, fresh_len, fresh_kv, page_pool, queries, stores, tps):
    slots, _, page, width = page_pool.shape
    block_rows, columns = queries.shape
    heads = columns // HD
    requests = fresh_len.shape[1]
    dt = page_pool.dtype
    items = block_rows // ROWS + requests - 1
    stack = ROWS * heads
    smem = pl.BlockSpec(memory_space=pltpu.SMEM)
    vmem = pl.BlockSpec(memory_space=pltpu.VMEM)
    any_spec = pl.BlockSpec(memory_space=pl.ANY)
    sem = pltpu.SemaphoreType.DMA
    return pl.pallas_call(
        functools.partial(exchange_kernel, stores, tps, heads),
        out_shape=(
            jax.ShapeDtypeStruct((stores + tps, 2, page, width), dt),
            jax.ShapeDtypeStruct((stores, 2, page, width), dt),
            jax.ShapeDtypeStruct((items, stack, 2 * HD), jnp.float32),
        ),
        in_specs=[smem, smem, any_spec, any_spec, any_spec, any_spec],
        out_specs=(vmem, any_spec, any_spec),
        scratch_shapes=[
            pltpu.VMEM((stores, 1, LANES), jnp.int32),
            pltpu.SMEM((stores, 1, LANES), jnp.int32),
            pltpu.VMEM((slots, 2, page, width), dt),
            pltpu.VMEM((2, stores, 2, page, width), dt),
            pltpu.VMEM((block_rows // ROWS, ROWS, columns), dt),
            pltpu.VMEM((stack, HD), jnp.bfloat16),
            pltpu.VMEM((EARLY // 2, stack, 2 * PAGE), jnp.float32),
            pltpu.VMEM((2, stack, 2 * HD), jnp.float32),
            sem((7,)),
            sem((2,)),
            sem((block_rows // ROWS,)),
            sem((stores,)),
            sem((stores,)),
            sem((2, stores)),
            sem((2, stores)),
            sem((tps,)),
            sem((tps,)),
        ],
        compiler_params=pltpu.CompilerParams(
            collective_id=0, has_side_effects=True, vmem_limit_bytes=36 << 20
        ),
        name="exchange",
    )(plan, fresh_len, want, fresh_kv, page_pool, queries)


def finish_kernel(
    heads, plan_s, length_s, q_ref, state_ref, pages_ref, late_ref, out_ref,
    late, row_id, scores, state, sem, state_sem,
):
    requests = length_s.shape[1]
    stack = ROWS * heads
    stores = late.shape[0]
    entries = (plan_s.shape[0] - 2 * requests) // 2
    pages = entries // requests
    copy = pltpu.make_async_copy(late_ref, late, sem)
    copy.start()
    items = state_ref.shape[0]

    def state_copy(item):
        slot = item % 2
        return pltpu.make_async_copy(state_ref.at[item], state.at[slot], state_sem.at[slot])

    state_copy(0).start()
    row_id[...] = one_hot_rows(stack)
    out_row = lax.broadcasted_iota(jnp.int32, (ROWS, HD), 0)
    copy.wait()

    def one_request(r, carry):
        offset, item0 = carry
        length = length_s[0, r]
        n0 = plan_s[2 * entries + r]
        n1 = plan_s[2 * entries + requests + r]
        b0 = offset // ROWS
        b1 = (offset + length - 1) // ROWS + 1

        def one_block(b, c):
            row0 = pl.multiple_of(b * ROWS, ROWS)
            item = item0 + b - b0
            slot = item % 2
            state_copy(item).wait()

            @pl.when(item + 1 < items)
            def _():
                state_copy(item + 1).start()

            f0 = offset // PAGE
            new = (row0 + (ROWS - 1)) // PAGE + 1 - f0
            done = jnp.minimum(new + n0, EARLY) - new
            left = n0 - done + n1
            mine = (out_row + row0 >= offset) & (out_row + row0 < offset + length)

            def entry(i):
                j = done + i
                late_one = j >= n0
                code = jnp.where(
                    late_one,
                    plan_s[entries + r * pages + jnp.minimum(j - n0, pages - 1) * jnp.where(late_one, 1, 0)],
                    plan_s[r * pages + jnp.minimum(j, pages - 1)],
                )
                used = i < left
                return late_one, jnp.where(used, code // 256, 0), jnp.where(used, code % 256, 0)

            def page(i, half):
                late_one, place, valid = entry(i)
                return jnp.where(late_one, late[place, half], pages_ref[place, half]), valid

            def key(i):
                k, valid = page(i, 0)
                return [k, page_mask(0, valid - 1, 0)]

            def value(i):
                return page(i, 1)[0]

            def variant(chunks):
                def body():
                    acc = state[slot, :, :HD]
                    sums = state[slot, :, HD:]
                    total = jnp.broadcast_to(sums[:, :1], (stack, HD))
                    if chunks:
                        old = sums[:, HD // 2:HD // 2 + 1]
                        q = stacked(q_ref[pl.ds(row0, ROWS), :], row_id[...], heads)
                        top, mixed = attend_pages(
                            q,
                            [functools.partial(key, i) for i in range(2 * chunks)],
                            [functools.partial(value, i) for i in range(2 * chunks)],
                            scores, old,
                        )
                        fade = jnp.broadcast_to(jnp.exp2(old - top), (stack, HD))
                        acc = acc * fade + mixed[:, :HD]
                        total = total * fade + mixed[:, HD:]
                    result = (acc / total).astype(jnp.bfloat16)
                    for h in range(heads):
                        at = (pl.ds(row0, ROWS), slice(h * HD, (h + 1) * HD))
                        out_ref[at] = jnp.where(
                            mine, result[h * ROWS:(h + 1) * ROWS], out_ref[at]
                        )
                return body

            chunks = (left + 1) // 2
            for n in range(pages // 2 + 1):
                pl.when(chunks == n)(variant(n))
            return c

        lax.fori_loop(b0, b1, one_block, 0)
        return offset + length, item0 + b1 - b0

    _, used_items = lax.fori_loop(0, requests, one_request, (0, 0))

    @pl.when(used_items < items)
    def _():
        state_copy(used_items).wait()


def finish(plan, fresh_len, queries, state, pages, late):
    block_rows, columns = queries.shape
    heads = columns // HD
    stack = ROWS * heads
    smem = pl.BlockSpec(memory_space=pltpu.SMEM)
    vmem = pl.BlockSpec(memory_space=pltpu.VMEM)
    return pl.pallas_call(
        functools.partial(finish_kernel, heads),
        out_shape=jax.ShapeDtypeStruct((block_rows, columns), queries.dtype),
        in_specs=[smem, smem, vmem, pl.BlockSpec(memory_space=pl.ANY), vmem, pl.BlockSpec(memory_space=pl.ANY)],
        out_specs=vmem,
        scratch_shapes=[
            pltpu.VMEM(late.shape, late.dtype),
            pltpu.VMEM((stack, HD), jnp.bfloat16),
            pltpu.VMEM((4, stack, 2 * PAGE), jnp.float32),
            pltpu.VMEM((2, stack, 2 * HD), jnp.float32),
            pltpu.SemaphoreType.DMA,
            pltpu.SemaphoreType.DMA((2,)),
        ],
        compiler_params=pltpu.CompilerParams(vmem_limit_bytes=30 << 20),
        name="finish",
    )(plan, fresh_len, queries, state, pages, late)


def in_hbm(x):
    return pltpu.with_memory_space_constraint(x, pltpu.HBM)


def local(queries, fresh_kv, page_pool, page_host, page_slot, prefix_len, fresh_len):
    stores = lax.axis_size("store")
    tps = lax.axis_size("tp")
    want, plan = make_plan(page_host, page_slot, prefix_len, stores)
    pages, late, state = exchange(
        plan, want, fresh_len, in_hbm(fresh_kv), in_hbm(page_pool), in_hbm(queries), stores, tps
    )
    return finish(plan, fresh_len, queries, state, pages, late)


def solution(mesh):
    placed = (
        P("store", "tp"),
        P(None, ("store", "tp"), None),
        P("store", None, None, "tp"),
        P("store", None),
        P("store", None),
        P("store"),
        P("store", None),
    )
    return jax.shard_map(
        local, mesh=mesh, in_specs=placed, out_specs=P("store", "tp"), check_vma=False
    )
```

```python
import functools
import math

import jax
import jax.numpy as jnp
from jax import lax
from jax.experimental import pallas as pl
from jax.experimental.pallas import tpu as pltpu
from jax.sharding import PartitionSpec as P

HD = 128
PAGE = 128
LANES = 128
PAGES_MAX = 8
NEG = -1e30
FAR = 1 << 20
MESH = pl.DeviceIdType.MESH
RING = 8
ROWS = 64
MIDDLE = 2
MOST_NEW = 384
NEAR = 2
SCALE = math.log2(math.e) / math.sqrt(HD)


def plan_kernel(host_s, slot_s, prefix_s, length_s, want_ref, plan_out, want_s, count, sem):
    requests, pages = host_s.shape
    stores = count.shape[0]
    entries = requests * pages
    my_z = lax.axis_index("store") % RING

    def clear(i, c):
        count[i] = 0
        want_s[i, 0, 0] = 0
        want_s[i, 0, 1] = 0
        return c

    lax.fori_loop(0, stores, clear, 0)

    def put(at, value):
        want_s[stores, 0, at] = value
        plan_out[at] = value

    for r in range(requests):
        prefix = prefix_s[r]

        def one(p, c):
            n0, n1, n2 = c
            host = host_s[r, p]
            rank = jnp.minimum(count[host], 1)
            count[host] = rank + 1
            want_s[host, 0, rank] = slot_s[r, p]
            away = (host + RING - my_z) % RING
            far = jnp.where((away > NEAR) & (away < RING - NEAR), rank, 0)
            group = rank + far
            at = group * entries + r * pages + jnp.where(rank == 0, n0, jnp.where(far == 0, n1, n2))
            put(at, host * 256 + jnp.minimum(prefix - p * PAGE, PAGE))
            return n0 + 1 - rank, n1 + rank - far, n2 + far

        counts = lax.fori_loop(0, lax.div(prefix + (PAGE - 1), PAGE), one, (0, 0, 0))
        for group in range(3):
            put(3 * entries + group * requests + r, counts[group])
        put(3 * entries + 3 * requests + r, length_s[0, r])
    copy = pltpu.make_async_copy(want_s, want_ref, sem)
    copy.start()
    copy.wait()


def make_plan(page_host, page_slot, prefix_len, fresh_len, stores):
    smem = pl.BlockSpec(memory_space=pltpu.SMEM)
    return pl.pallas_call(
        plan_kernel,
        out_shape=(
            jax.ShapeDtypeStruct((stores + 1, 1, LANES), jnp.int32),
            jax.ShapeDtypeStruct((LANES,), jnp.int32),
        ),
        in_specs=[smem, smem, smem, smem],
        out_specs=(pl.BlockSpec(memory_space=pl.ANY), smem),
        scratch_shapes=[
            pltpu.SMEM((stores + 1, 1, LANES), jnp.int32),
            pltpu.SMEM((stores,), jnp.int32),
            pltpu.SemaphoreType.DMA,
        ],
        name="plan",
    )(page_host, page_slot, prefix_len, fresh_len)


class Plan:
    def __init__(self, get, requests, pages):
        self.get, self.requests, self.pages = get, requests, pages
        self.entries = requests * pages

    def size(self, group, r):
        return self.get(3 * self.entries + group * self.requests + r)

    def length(self, r):
        return self.get(3 * self.entries + 3 * self.requests + r)

    def item(self, item):
        offset = start = r = row0 = at = 0
        for q in range(self.requests):
            length = self.length(q)
            first = offset // ROWS
            count = (offset + length - 1) // ROWS - first + 1
            here = item >= start
            block = jnp.maximum(first + jnp.minimum(item - start, count - 1), 0)
            r = jnp.where(here, q, r)
            row0 = jnp.where(here, block * ROWS, row0)
            at = jnp.where(here, offset, at)
            start = start + count
            offset = offset + length
        return r, row0, at

    def page(self, group, r, i):
        used = i < self.size(group, r)
        code = self.get(
            group * self.entries + r * self.pages + jnp.clip(i, 0, self.pages - 1)
        )
        return jnp.where(used, code // 256, 0), jnp.where(used, code % 256, 0)


def one_hot_rows(stack):
    lane = lax.broadcasted_iota(jnp.int32, (stack, HD), 1)
    row = lax.rem(lax.broadcasted_iota(jnp.int32, (stack, HD), 0), ROWS)
    return (lane == row).astype(jnp.bfloat16)


def stacked(q, row_id, heads):
    q = jnp.concatenate([q[:, h * HD:(h + 1) * HD] for h in range(heads)], axis=0)
    return jnp.concatenate([q, row_id], axis=1)


def page_mask(low, high, slope):
    key = lax.broadcasted_iota(jnp.int32, (PAGE, HD), 0)
    lane = lax.broadcasted_iota(jnp.int32, (PAGE, HD), 1)
    ok = (key >= low) & (key <= high + lane * slope)
    return jnp.where(ok, 0.0, NEG).astype(jnp.bfloat16)


def attend_pages(q, keys, values, scores, top):
    chunks = len(keys) // 2
    ones = jnp.ones((PAGE, HD), jnp.bfloat16)
    for j in range(chunks):
        k = jnp.concatenate(
            [jnp.concatenate(keys[i](), axis=1) for i in (2 * j, 2 * j + 1)], axis=0
        )
        scores[j] = lax.dot_general(
            q, k, (((1,), (1,)), ((), ())), preferred_element_type=jnp.float32
        )
    best = scores[0]
    for j in range(1, chunks):
        best = jnp.maximum(best, scores[j])
    best = jnp.max(jnp.maximum(best[:, :PAGE], best[:, PAGE:]), axis=1, keepdims=True) * SCALE
    best = jnp.broadcast_to(best, (q.shape[0], HD))
    top = best if top is None else jnp.maximum(top, best)
    mixed = None
    for j in range(chunks):
        w = jnp.concatenate(
            [
                jnp.exp2(scores[j, :, half * PAGE:(half + 1) * PAGE] * SCALE - top)
                for half in range(2)
            ],
            axis=1,
        ).astype(jnp.bfloat16)
        v = jnp.concatenate(
            [jnp.concatenate([values[i](), ones], axis=1) for i in (2 * j, 2 * j + 1)], axis=0
        )
        part = jnp.dot(w, v, preferred_element_type=jnp.float32)
        mixed = part if mixed is None else mixed + part
    return top, mixed


def merged(old_acc, old_total, old_top, top, mixed):
    fade = jnp.exp2(old_top - top)
    return old_acc * fade + mixed[:, :HD], old_total * fade + mixed[:, HD:]


def exchange_kernel(
    stores, tps, heads, requests, want, fresh_ref, pool_ref, q_ref,
    near_ref, far_ref, state,
    got, got_s, plan_s, new_ref, pages_ref, pool_v, send_v, q_v, row_id, masks, scores,
    local_sem, q_sem, want_send, want_recv, page_send, page_recv, new_send, new_recv,
):
    me = lax.axis_index("store")
    mt = lax.axis_index("tp")
    my_y, my_z = me // RING, me % RING
    columns = stores // RING
    items = state.shape[0]
    stack = ROWS * heads
    blocks = q_v.shape[0]
    plan = Plan(lambda i: plan_s[0, i], requests, PAGES_MAX)

    def local_copy(src, dst, n):
        return pltpu.make_async_copy(src, dst, local_sem.at[n])

    def q_copy(i):
        return pltpu.make_async_copy(
            q_ref.at[pl.ds(pl.multiple_of(i * ROWS, ROWS), ROWS), :], q_v.at[i], q_sem.at[i]
        )

    def run(start, stop, body):
        def step(i, c):
            body(i)
            return c
        lax.fori_loop(start, stop, step, 0)

    def partner(i):
        turn = i // columns
        half = (turn + 1) // 2
        odd = turn % 2
        dz = odd * half + (1 - odd) * (RING - half)
        return ((my_y + i % columns) % columns) * RING + (my_z + dz) % RING

    last_near = (2 * NEAR + 1) * columns
    barrier = pltpu.get_barrier_semaphore()

    def greet(axis, d):
        pl.semaphore_signal(barrier, inc=1, device_id={axis: d}, device_id_type=MESH)

    run(1, stores, lambda i: greet("store", partner(i)))
    run(1, tps, lambda i: greet("tp", (mt + i) % tps))

    pool_copy = local_copy(pool_ref, pool_v, 0)
    pool_copy.start()
    own_new = local_copy(
        fresh_ref.at[:, :, pl.ds(pl.multiple_of(mt * HD, HD), HD)], new_ref.at[mt], 1
    )
    own_new.start()
    plan_copy = local_copy(want.at[stores], plan_s, 2)
    plan_copy.start()
    got_own = local_copy(want.at[me], got.at[me], 3)
    got_own.start()
    run(0, blocks, lambda i: q_copy(i).start())
    pl.semaphore_wait(barrier, stores - 1 + tps - 1)

    def remote(src, dst, send, recv, axis, d):
        return pltpu.make_async_remote_copy(
            src_ref=src, dst_ref=dst, send_sem=send, recv_sem=recv,
            device_id={axis: d}, device_id_type=MESH,
        )

    def new_copy(i):
        d = (mt + i) % tps
        return remote(
            fresh_ref.at[:, :, pl.ds(pl.multiple_of(d * HD, HD), HD)],
            new_ref.at[mt], new_send.at[i], new_recv.at[i], "tp", d,
        )

    def want_copy(i):
        d = partner(i)
        return remote(want.at[d], got.at[me], want_send.at[i], want_recv.at[i], "store", d)

    def page_copy(k, dst, i):
        d = partner(i)
        return remote(
            send_v.at[k, d], dst.at[me], page_send.at[k, i], page_recv.at[k, i], "store", d
        )

    run(1, stores, lambda i: want_copy(i).start())
    run(1, tps, lambda i: new_copy(i).start())
    row_id[...] = one_hot_rows(stack)
    got_own.wait()
    run(1, stores, lambda i: want_copy(i).wait())
    scalars = local_copy(got, got_s, 4)
    scalars.start()
    pool_copy.wait()
    scalars.wait()

    def pack_send(k, dst):
        def body(i):
            d = partner(i)
            send_v[k, d] = pool_v[got_s[d, 0, k]]
            page_copy(k, dst, i).start()
        return body

    run(1, stores, pack_send(0, pages_ref))
    run(1, last_near, pack_send(1, near_ref))
    run(last_near, stores, pack_send(1, far_ref))
    own = []
    for k, dst in enumerate((pages_ref, near_ref)):
        send_v[k, me] = pool_v[got_s[me, 0, k]]
        own.append(local_copy(send_v.at[k, me], dst.at[me], 5 + k))
        own[k].start()
    for copy in own:
        copy.wait()
    own_new.wait()
    plan_copy.wait()
    run(0, blocks, lambda i: q_copy(i).wait())
    run(1, tps, lambda i: new_copy(i).wait())

    pages = plan.pages

    def first_mask(i):
        _, valid = plan.page(0, i // pages, i % pages)
        masks[i] = page_mask(0, valid - 1, 0)

    def second_mask(i):
        _, valid = plan.page(1, i // MIDDLE, i % MIDDLE)
        masks[requests * pages + i] = page_mask(0, valid - 1, 0)

    run(0, requests * pages, first_mask)
    run(0, requests * MIDDLE, second_mask)

    def stacked_rows(row0):
        return stacked(q_v[jnp.clip(row0 // ROWS, 0, blocks - 1)], row_id[...], heads)

    def save(item, acc, total, top):
        state[item, :, :HD] = acc
        state[item, :, HD:2 * HD] = total
        state[item, :, 2 * HD:] = top

    def new_item(item):
        r, row0, offset = plan.item(item)
        f0 = offset // PAGE
        new = (row0 + (ROWS - 1)) // PAGE + 1 - f0

        def place(i):
            return jnp.clip(f0 + i, 0, tps - 1)

        def key(i):
            base = PAGE * (f0 + i)
            low = jnp.where(i < new, offset - base, FAR)
            return [new_ref[place(i), 0], page_mask(low, row0 - base, 1)]

        count = 2 * ((MOST_NEW + PAGE - 2) // PAGE // 2 + 1)
        top, mixed = attend_pages(
            stacked_rows(row0),
            [functools.partial(key, i) for i in range(count)],
            [lambda i=i: new_ref[place(i), 1] for i in range(count)],
            scores, None,
        )
        save(item, mixed[:, :HD], mixed[:, HD:], top)

    def more(item, ref, group, first_mask_at, count):
        r, row0, _ = plan.item(item)

        def place(i):
            host, valid = plan.page(group, r, i)
            return jnp.clip(jnp.where(valid > 0, host, me), 0, stores - 1)

        acc = state[item, :, :HD]
        old = state[item, :, 2 * HD:]
        top, mixed = attend_pages(
            stacked_rows(row0),
            [lambda i=i: [ref[place(i), 0], masks[first_mask_at + r * count + i]] for i in range(count)],
            [lambda i=i: ref[place(i), 1] for i in range(count)],
            scores, old,
        )
        acc, total = merged(acc, state[item, :, HD:2 * HD], old, top, mixed)
        save(item, acc, total, top)

    run(0, items, new_item)
    run(1, stores, lambda i: page_copy(0, pages_ref, i).wait())
    run(0, items, lambda item: more(item, pages_ref, 0, 0, pages))
    run(1, last_near, lambda i: page_copy(1, near_ref, i).wait())
    run(0, items, lambda item: more(item, near_ref, 1, requests * pages, MIDDLE))
    run(last_near, stores, lambda i: page_copy(1, far_ref, i).wait())


def exchange(want, fresh_kv, page_pool, queries, requests, stores, tps):
    slots, _, page, width = page_pool.shape
    block_rows, columns = queries.shape
    heads = columns // HD
    dt = page_pool.dtype
    items = block_rows // ROWS + requests - 1
    stack = ROWS * heads
    vmem = pl.BlockSpec(memory_space=pltpu.VMEM)
    any_spec = pl.BlockSpec(memory_space=pl.ANY)
    sem = pltpu.SemaphoreType.DMA
    return pl.pallas_call(
        functools.partial(exchange_kernel, stores, tps, heads, requests),
        out_shape=(
            jax.ShapeDtypeStruct((stores, 2, page, width), dt),
            jax.ShapeDtypeStruct((stores, 2, page, width), dt),
            jax.ShapeDtypeStruct((items, stack, 3 * HD), jnp.float32),
        ),
        in_specs=[any_spec, any_spec, any_spec, any_spec],
        out_specs=(vmem, any_spec, vmem),
        scratch_shapes=[
            pltpu.VMEM((stores, 1, LANES), jnp.int32),
            pltpu.SMEM((stores, 1, LANES), jnp.int32),
            pltpu.SMEM((1, LANES), jnp.int32),
            pltpu.VMEM((tps, 2, page, width), dt),
            pltpu.VMEM((stores, 2, page, width), dt),
            pltpu.VMEM((slots, 2, page, width), dt),
            pltpu.VMEM((2, stores, 2, page, width), dt),
            pltpu.VMEM((block_rows // ROWS, ROWS, columns), dt),
            pltpu.VMEM((stack, HD), jnp.bfloat16),
            pltpu.VMEM((requests * (PAGES_MAX + MIDDLE), PAGE, HD), jnp.bfloat16),
            pltpu.VMEM((PAGES_MAX // 2, stack, 2 * PAGE), jnp.float32),
            sem((7,)),
            sem((block_rows // ROWS,)),
            sem((stores,)),
            sem((stores,)),
            sem((2, stores)),
            sem((2, stores)),
            sem((tps,)),
            sem((tps,)),
        ],
        compiler_params=pltpu.CompilerParams(
            collective_id=0, has_side_effects=True, vmem_limit_bytes=28 << 20
        ),
        name="exchange",
    )(want, fresh_kv, page_pool, queries)


def finish_kernel(
    heads, requests, plan_s, q_ref, state, near_ref, far_v, out_ref,
    out_v, row_id, scores, out_sem,
):
    own = lax.axis_index("store")
    stack = ROWS * heads
    blocks = out_v.shape[0]
    plan = Plan(lambda i: plan_s[i], requests, PAGES_MAX)
    def out_copy(b):
        return pltpu.make_async_copy(
            out_v.at[b], out_ref.at[pl.ds(pl.multiple_of(b * ROWS, ROWS), ROWS), :], out_sem.at[b]
        )

    row_id[...] = one_hot_rows(stack)
    out_row = lax.broadcasted_iota(jnp.int32, (ROWS, HD), 0)

    def one_request(r, carry):
        offset, item0 = carry
        length = plan.length(r)
        over = jnp.maximum(plan.size(1, r) - MIDDLE, 0)
        left = over + plan.size(2, r)
        b0 = offset // ROWS
        b1 = (offset + length - 1) // ROWS + 1

        def one_block(b, c):
            row0 = pl.multiple_of(b * ROWS, ROWS)
            item = item0 + b - b0
            mine = (out_row + row0 >= offset) & (out_row + row0 < offset + length)

            def page(i, half):
                is_near = i < over
                near_host, near_valid = plan.page(1, r, MIDDLE + i)
                far_host, far_valid = plan.page(2, r, i - over)
                use_near = is_near | (i >= left)
                data = jnp.where(
                    use_near,
                    near_ref[jnp.where(is_near, near_host, own), half],
                    far_v[jnp.where(use_near, 0, far_host), half],
                )
                valid = jnp.where(is_near, near_valid, jnp.where(i < left, far_valid, 0))
                return data, valid

            def key(i):
                k, valid = page(i, 0)
                return [k, page_mask(0, valid - 1, 0)]

            def variant(chunks):
                def body():
                    acc = state[item, :, :HD]
                    total = state[item, :, HD:2 * HD]
                    if chunks:
                        old = state[item, :, 2 * HD:]
                        q = stacked(q_ref[pl.ds(row0, ROWS), :], row_id[...], heads)
                        top, mixed = attend_pages(
                            q,
                            [functools.partial(key, i) for i in range(2 * chunks)],
                            [lambda i=i: page(i, 1)[0] for i in range(2 * chunks)],
                            scores, old,
                        )
                        acc, total = merged(acc, total, old, top, mixed)
                    result = (acc / total).astype(jnp.bfloat16)
                    for h in range(heads):
                        at = (b, slice(None), slice(h * HD, (h + 1) * HD))
                        out_v[at] = jnp.where(mine, result[h * ROWS:(h + 1) * ROWS], out_v[at])
                return body

            chunks = (left + 1) // 2
            for n in range(PAGES_MAX // 2 + 1):
                pl.when(chunks == n)(variant(n))

            @pl.when(offset + length >= row0 + ROWS)
            def _():
                out_copy(b).start()

            return c

        lax.fori_loop(b0, b1, one_block, 0)
        return offset + length, item0 + b1 - b0

    lax.fori_loop(0, requests, one_request, (0, 0))

    def wait_out(b, c):
        out_copy(b).wait()
        return c

    lax.fori_loop(0, blocks, wait_out, 0)


def finish(plan, queries, state, near, far, requests):
    block_rows, columns = queries.shape
    heads = columns // HD
    stack = ROWS * heads
    smem = pl.BlockSpec(memory_space=pltpu.SMEM)
    vmem = pl.BlockSpec(memory_space=pltpu.VMEM)
    any_spec = pl.BlockSpec(memory_space=pl.ANY)
    return pl.pallas_call(
        functools.partial(finish_kernel, heads, requests),
        out_shape=jax.ShapeDtypeStruct((block_rows, columns), queries.dtype),
        in_specs=[smem, vmem, vmem, vmem, vmem],
        out_specs=any_spec,
        scratch_shapes=[
            pltpu.VMEM((block_rows // ROWS, ROWS, columns), queries.dtype),
            pltpu.VMEM((stack, HD), jnp.bfloat16),
            pltpu.VMEM((PAGES_MAX // 2, stack, 2 * PAGE), jnp.float32),
            pltpu.SemaphoreType.DMA((block_rows // ROWS,)),
        ],
        compiler_params=pltpu.CompilerParams(vmem_limit_bytes=16 << 20),
        name="finish",
    )(plan, queries, state, near, far)


def in_hbm(x):
    return pltpu.with_memory_space_constraint(x, pltpu.HBM)


def local(queries, fresh_kv, page_pool, page_host, page_slot, prefix_len, fresh_len):
    stores = lax.axis_size("store")
    tps = lax.axis_size("tp")
    requests = page_host.shape[0]
    want, plan = make_plan(page_host, page_slot, prefix_len, fresh_len, stores)
    near, far, state = exchange(
        in_hbm(want), in_hbm(fresh_kv), in_hbm(page_pool), in_hbm(queries), requests, stores, tps
    )
    return finish(plan, queries, state, near, far, requests)


def solution(mesh):
    placed = (
        P("store", "tp"),
        P(None, ("store", "tp"), None),
        P("store", None, None, "tp"),
        P("store", None),
        P("store", None),
        P("store"),
        P("store", None),
    )
    return jax.shard_map(
        local, mesh=mesh, in_specs=placed, out_specs=P("store", "tp"), check_vma=False
    )
```

```python
import functools
import math

import jax
import jax.numpy as jnp
from jax import lax
from jax.experimental import pallas as pl
from jax.experimental.pallas import tpu as pltpu
from jax.sharding import PartitionSpec as P

HD = 128
PAGE = 128
LANES = 128
PAGES_MAX = 8
NEG = -1e30
FAR = 1 << 20
MESH = pl.DeviceIdType.MESH
RING = 8
ROWS = 64
MIDDLE = 2
MOST_NEW = 384
NEAR = 2
SCALE = math.log2(math.e) / math.sqrt(HD)


def plan_kernel(host_s, slot_s, prefix_s, length_s, want_ref, plan_out, want_s, count, sem):
    requests, pages = host_s.shape
    stores = count.shape[0]
    entries = requests * pages
    my_z = lax.axis_index("store") % RING

    def clear(i, c):
        count[i] = 0
        want_s[i, 0, 0] = 0
        want_s[i, 0, 1] = 0
        return c

    lax.fori_loop(0, stores, clear, 0)

    def put(at, value):
        want_s[stores, 0, at] = value
        plan_out[at] = value

    for r in range(requests):
        prefix = prefix_s[r]

        def one(p, c):
            n0, n1, n2 = c
            host = host_s[r, p]
            rank = jnp.minimum(count[host], 1)
            count[host] = rank + 1
            want_s[host, 0, rank] = slot_s[r, p]
            away = (host + RING - my_z) % RING
            far = jnp.where((away > NEAR) & (away < RING - NEAR), rank, 0)
            group = rank + far
            at = group * entries + r * pages + jnp.where(rank == 0, n0, jnp.where(far == 0, n1, n2))
            put(at, host * 256 + jnp.minimum(prefix - p * PAGE, PAGE))
            return n0 + 1 - rank, n1 + rank - far, n2 + far

        counts = lax.fori_loop(0, lax.div(prefix + (PAGE - 1), PAGE), one, (0, 0, 0))
        for group in range(3):
            put(3 * entries + group * requests + r, counts[group])
        put(3 * entries + 3 * requests + r, length_s[0, r])
    copy = pltpu.make_async_copy(want_s, want_ref, sem)
    copy.start()
    copy.wait()


def make_plan(page_host, page_slot, prefix_len, fresh_len, stores):
    smem = pl.BlockSpec(memory_space=pltpu.SMEM)
    return pl.pallas_call(
        plan_kernel,
        out_shape=(
            jax.ShapeDtypeStruct((stores + 1, 1, LANES), jnp.int32),
            jax.ShapeDtypeStruct((LANES,), jnp.int32),
        ),
        in_specs=[smem, smem, smem, smem],
        out_specs=(pl.BlockSpec(memory_space=pl.ANY), smem),
        scratch_shapes=[
            pltpu.SMEM((stores + 1, 1, LANES), jnp.int32),
            pltpu.SMEM((stores,), jnp.int32),
            pltpu.SemaphoreType.DMA,
        ],
        name="plan",
    )(page_host, page_slot, prefix_len, fresh_len)


class Plan:
    def __init__(self, get, requests, pages):
        self.get, self.requests, self.pages = get, requests, pages
        self.entries = requests * pages

    def size(self, group, r):
        return self.get(3 * self.entries + group * self.requests + r)

    def length(self, r):
        return self.get(3 * self.entries + 3 * self.requests + r)

    def item(self, item):
        offset = start = r = row0 = at = 0
        for q in range(self.requests):
            length = self.length(q)
            first = offset // ROWS
            count = (offset + length - 1) // ROWS - first + 1
            here = item >= start
            block = jnp.maximum(first + jnp.minimum(item - start, count - 1), 0)
            r = jnp.where(here, q, r)
            row0 = jnp.where(here, block * ROWS, row0)
            at = jnp.where(here, offset, at)
            start = start + count
            offset = offset + length
        return r, row0, at

    def page(self, group, r, i):
        used = i < self.size(group, r)
        code = self.get(
            group * self.entries + r * self.pages + jnp.clip(i, 0, self.pages - 1)
        )
        return jnp.where(used, code // 256, 0), jnp.where(used, code % 256, 0)


def one_hot_rows(stack):
    lane = lax.broadcasted_iota(jnp.int32, (stack, HD), 1)
    row = lax.rem(lax.broadcasted_iota(jnp.int32, (stack, HD), 0), ROWS)
    return (lane == row).astype(jnp.bfloat16)


def stacked(q, row_id, heads):
    q = jnp.concatenate([q[:, h * HD:(h + 1) * HD] for h in range(heads)], axis=0)
    return jnp.concatenate([q, row_id], axis=1)


def page_mask(low, high, slope):
    key = lax.broadcasted_iota(jnp.int32, (PAGE, HD), 0)
    lane = lax.broadcasted_iota(jnp.int32, (PAGE, HD), 1)
    ok = (key >= low) & (key <= high + lane * slope)
    return jnp.where(ok, 0.0, NEG).astype(jnp.bfloat16)


def attend_pages(q, keys, values, scores, top):
    chunks = len(keys) // 2
    ones = jnp.ones((PAGE, HD), jnp.bfloat16)
    for j in range(chunks):
        k = jnp.concatenate(
            [jnp.concatenate(keys[i](), axis=1) for i in (2 * j, 2 * j + 1)], axis=0
        )
        scores[j] = lax.dot_general(
            q, k, (((1,), (1,)), ((), ())), preferred_element_type=jnp.float32
        )
    best = scores[0]
    for j in range(1, chunks):
        best = jnp.maximum(best, scores[j])
    best = jnp.max(jnp.maximum(best[:, :PAGE], best[:, PAGE:]), axis=1, keepdims=True) * SCALE
    best = jnp.broadcast_to(best, (q.shape[0], HD))
    top = best if top is None else jnp.maximum(top, best)
    mixed = None
    for j in range(chunks):
        w = jnp.concatenate(
            [
                jnp.exp2(scores[j, :, half * PAGE:(half + 1) * PAGE] * SCALE - top)
                for half in range(2)
            ],
            axis=1,
        ).astype(jnp.bfloat16)
        v = jnp.concatenate(
            [jnp.concatenate([values[i](), ones], axis=1) for i in (2 * j, 2 * j + 1)], axis=0
        )
        part = jnp.dot(w, v, preferred_element_type=jnp.float32)
        mixed = part if mixed is None else mixed + part
    return top, mixed


def merged(old_acc, old_total, old_top, top, mixed):
    fade = jnp.exp2(old_top - top)
    return old_acc * fade + mixed[:, :HD], old_total * fade + mixed[:, HD:]


def exchange_kernel(
    stores, tps, heads, requests, want, fresh_ref, pool_ref, q_ref,
    near_ref, far_ref, state,
    got_s, plan_s, new_ref, pages_ref, pool_v, send_v, q_v, row_id, masks, scores,
    local_sem, q_sem, want_send, want_recv, page_send, page_recv, new_send, new_recv,
):
    me = lax.axis_index("store")
    mt = lax.axis_index("tp")
    my_y, my_z = me // RING, me % RING
    columns = stores // RING
    items = state.shape[0]
    stack = ROWS * heads
    blocks = q_v.shape[0]
    plan = Plan(lambda i: plan_s[0, i], requests, PAGES_MAX)

    def local_copy(src, dst, n):
        return pltpu.make_async_copy(src, dst, local_sem.at[n])

    def q_copy(i):
        return pltpu.make_async_copy(
            q_ref.at[pl.ds(pl.multiple_of(i * ROWS, ROWS), ROWS), :], q_v.at[i], q_sem.at[i]
        )

    def run(start, stop, body):
        def step(i, c):
            body(i)
            return c
        lax.fori_loop(start, stop, step, 0)

    def partner(i):
        turn = i // columns
        half = (turn + 1) // 2
        odd = turn % 2
        dz = odd * half + (1 - odd) * (RING - half)
        return ((my_y + i % columns) % columns) * RING + (my_z + dz) % RING

    last_near = (2 * NEAR + 1) * columns
    barrier = pltpu.get_barrier_semaphore()

    def greet(axis, d):
        pl.semaphore_signal(barrier, inc=1, device_id={axis: d}, device_id_type=MESH)

    run(1, stores, lambda i: greet("store", partner(i)))
    run(1, tps, lambda i: greet("tp", (mt + i) % tps))

    pool_copy = local_copy(pool_ref, pool_v, 0)
    pool_copy.start()
    own_new = local_copy(
        fresh_ref.at[:, :, pl.ds(pl.multiple_of(mt * HD, HD), HD)], new_ref.at[mt], 1
    )
    own_new.start()
    plan_copy = local_copy(want.at[stores], plan_s, 2)
    plan_copy.start()
    got_own = local_copy(want.at[me], got_s.at[me], 3)
    got_own.start()
    run(0, blocks, lambda i: q_copy(i).start())
    pl.semaphore_wait(barrier, stores - 1 + tps - 1)

    def remote(src, dst, send, recv, axis, d):
        return pltpu.make_async_remote_copy(
            src_ref=src, dst_ref=dst, send_sem=send, recv_sem=recv,
            device_id={axis: d}, device_id_type=MESH,
        )

    def new_copy(i):
        d = (mt + i) % tps
        return remote(
            fresh_ref.at[:, :, pl.ds(pl.multiple_of(d * HD, HD), HD)],
            new_ref.at[mt], new_send.at[i], new_recv.at[i], "tp", d,
        )

    def want_copy(i):
        d = partner(i)
        return remote(want.at[d], got_s.at[me], want_send.at[i], want_recv.at[i], "store", d)

    def page_copy(k, dst, i):
        d = partner(i)
        return remote(
            send_v.at[k, d], dst.at[me], page_send.at[k, i], page_recv.at[k, i], "store", d
        )

    run(1, stores, lambda i: want_copy(i).start())
    run(1, tps, lambda i: new_copy(i).start())
    row_id[...] = one_hot_rows(stack)
    got_own.wait()
    run(1, stores, lambda i: want_copy(i).wait())
    pool_copy.wait()

    def pack_send(k, dst):
        def body(i):
            d = partner(i)
            send_v[k, d] = pool_v[got_s[d, 0, k]]
            page_copy(k, dst, i).start()
        return body

    run(1, stores, pack_send(0, pages_ref))
    run(1, last_near, pack_send(1, near_ref))
    run(last_near, stores, pack_send(1, far_ref))
    own = []
    for k, dst in enumerate((pages_ref, near_ref)):
        send_v[k, me] = pool_v[got_s[me, 0, k]]
        own.append(local_copy(send_v.at[k, me], dst.at[me], 5 + k))
        own[k].start()
    for copy in own:
        copy.wait()
    own_new.wait()
    plan_copy.wait()
    run(0, blocks, lambda i: q_copy(i).wait())
    run(1, tps, lambda i: new_copy(i).wait())

    pages = plan.pages

    def first_mask(i):
        _, valid = plan.page(0, i // pages, i % pages)
        masks[i] = page_mask(0, valid - 1, 0)

    def second_mask(i):
        _, valid = plan.page(1, i // MIDDLE, i % MIDDLE)
        masks[requests * pages + i] = page_mask(0, valid - 1, 0)

    run(0, requests * pages, first_mask)
    run(0, requests * MIDDLE, second_mask)

    def stacked_rows(row0):
        return stacked(q_v[jnp.clip(row0 // ROWS, 0, blocks - 1)], row_id[...], heads)

    def save(item, acc, total, top):
        state[item, :, :HD] = acc
        state[item, :, HD:2 * HD] = total
        state[item, :, 2 * HD:] = top

    def new_item(item):
        r, row0, offset = plan.item(item)
        f0 = offset // PAGE
        new = (row0 + (ROWS - 1)) // PAGE + 1 - f0

        def place(i):
            return jnp.clip(f0 + i, 0, tps - 1)

        def key(i):
            base = PAGE * (f0 + i)
            low = jnp.where(i < new, offset - base, FAR)
            return [new_ref[place(i), 0], page_mask(low, row0 - base, 1)]

        count = 2 * ((MOST_NEW + PAGE - 2) // PAGE // 2 + 1)
        top, mixed = attend_pages(
            stacked_rows(row0),
            [functools.partial(key, i) for i in range(count)],
            [lambda i=i: new_ref[place(i), 1] for i in range(count)],
            scores, None,
        )
        save(item, mixed[:, :HD], mixed[:, HD:], top)

    def more(item, ref, group, first_mask_at, count):
        r, row0, _ = plan.item(item)

        def place(i):
            host, valid = plan.page(group, r, i)
            return jnp.clip(jnp.where(valid > 0, host, me), 0, stores - 1)

        acc = state[item, :, :HD]
        old = state[item, :, 2 * HD:]
        top, mixed = attend_pages(
            stacked_rows(row0),
            [lambda i=i: [ref[place(i), 0], masks[first_mask_at + r * count + i]] for i in range(count)],
            [lambda i=i: ref[place(i), 1] for i in range(count)],
            scores, old,
        )
        acc, total = merged(acc, state[item, :, HD:2 * HD], old, top, mixed)
        save(item, acc, total, top)

    run(0, items, new_item)
    run(1, stores, lambda i: page_copy(0, pages_ref, i).wait())
    run(0, items, lambda item: more(item, pages_ref, 0, 0, pages))
    run(1, last_near, lambda i: page_copy(1, near_ref, i).wait())
    run(0, items, lambda item: more(item, near_ref, 1, requests * pages, MIDDLE))
    run(last_near, stores, lambda i: page_copy(1, far_ref, i).wait())


def exchange(want, fresh_kv, page_pool, queries, requests, stores, tps):
    slots, _, page, width = page_pool.shape
    block_rows, columns = queries.shape
    heads = columns // HD
    dt = page_pool.dtype
    items = block_rows // ROWS + requests - 1
    stack = ROWS * heads
    vmem = pl.BlockSpec(memory_space=pltpu.VMEM)
    any_spec = pl.BlockSpec(memory_space=pl.ANY)
    sem = pltpu.SemaphoreType.DMA
    return pl.pallas_call(
        functools.partial(exchange_kernel, stores, tps, heads, requests),
        out_shape=(
            jax.ShapeDtypeStruct((stores, 2, page, width), dt),
            jax.ShapeDtypeStruct((stores, 2, page, width), dt),
            jax.ShapeDtypeStruct((items, stack, 3 * HD), jnp.float32),
        ),
        in_specs=[any_spec, any_spec, any_spec, any_spec],
        out_specs=(vmem, any_spec, vmem),
        scratch_shapes=[
            pltpu.SMEM((stores, 1, LANES), jnp.int32),
            pltpu.SMEM((1, LANES), jnp.int32),
            pltpu.VMEM((tps, 2, page, width), dt),
            pltpu.VMEM((stores, 2, page, width), dt),
            pltpu.VMEM((slots, 2, page, width), dt),
            pltpu.VMEM((2, stores, 2, page, width), dt),
            pltpu.VMEM((block_rows // ROWS, ROWS, columns), dt),
            pltpu.VMEM((stack, HD), jnp.bfloat16),
            pltpu.VMEM((requests * (PAGES_MAX + MIDDLE), PAGE, HD), jnp.bfloat16),
            pltpu.VMEM((PAGES_MAX // 2, stack, 2 * PAGE), jnp.float32),
            sem((7,)),
            sem((block_rows // ROWS,)),
            sem((stores,)),
            sem((stores,)),
            sem((2, stores)),
            sem((2, stores)),
            sem((tps,)),
            sem((tps,)),
        ],
        compiler_params=pltpu.CompilerParams(
            collective_id=0, has_side_effects=True, vmem_limit_bytes=28 << 20
        ),
        name="exchange",
    )(want, fresh_kv, page_pool, queries)


def finish_kernel(
    heads, requests, plan_s, q_ref, state, near_ref, far_v, out_ref,
    out_v, row_id, scores, out_sem,
):
    own = lax.axis_index("store")
    stack = ROWS * heads
    blocks = out_v.shape[0]
    plan = Plan(lambda i: plan_s[i], requests, PAGES_MAX)
    def out_copy(b):
        return pltpu.make_async_copy(
            out_v.at[b], out_ref.at[pl.ds(pl.multiple_of(b * ROWS, ROWS), ROWS), :], out_sem.at[b]
        )

    row_id[...] = one_hot_rows(stack)
    out_row = lax.broadcasted_iota(jnp.int32, (ROWS, HD), 0)

    def one_request(r, carry):
        offset, item0 = carry
        length = plan.length(r)
        over = jnp.maximum(plan.size(1, r) - MIDDLE, 0)
        left = over + plan.size(2, r)
        b0 = offset // ROWS
        b1 = (offset + length - 1) // ROWS + 1

        def one_block(b, c):
            row0 = pl.multiple_of(b * ROWS, ROWS)
            item = item0 + b - b0
            mine = (out_row + row0 >= offset) & (out_row + row0 < offset + length)

            def page(i, half):
                is_near = i < over
                near_host, near_valid = plan.page(1, r, MIDDLE + i)
                far_host, far_valid = plan.page(2, r, i - over)
                use_near = is_near | (i >= left)
                data = jnp.where(
                    use_near,
                    near_ref[jnp.where(is_near, near_host, own), half],
                    far_v[jnp.where(use_near, 0, far_host), half],
                )
                valid = jnp.where(is_near, near_valid, jnp.where(i < left, far_valid, 0))
                return data, valid

            def key(i):
                k, valid = page(i, 0)
                return [k, page_mask(0, valid - 1, 0)]

            def variant(chunks):
                def body():
                    acc = state[item, :, :HD]
                    total = state[item, :, HD:2 * HD]
                    if chunks:
                        old = state[item, :, 2 * HD:]
                        q = stacked(q_ref[pl.ds(row0, ROWS), :], row_id[...], heads)
                        top, mixed = attend_pages(
                            q,
                            [functools.partial(key, i) for i in range(2 * chunks)],
                            [lambda i=i: page(i, 1)[0] for i in range(2 * chunks)],
                            scores, old,
                        )
                        acc, total = merged(acc, total, old, top, mixed)
                    result = (acc / total).astype(jnp.bfloat16)
                    for h in range(heads):
                        at = (b, slice(None), slice(h * HD, (h + 1) * HD))
                        out_v[at] = jnp.where(mine, result[h * ROWS:(h + 1) * ROWS], out_v[at])
                return body

            chunks = (left + 1) // 2
            for n in range(PAGES_MAX // 2 + 1):
                pl.when(chunks == n)(variant(n))

            @pl.when(offset + length >= row0 + ROWS)
            def _():
                out_copy(b).start()

            return c

        lax.fori_loop(b0, b1, one_block, 0)
        return offset + length, item0 + b1 - b0

    lax.fori_loop(0, requests, one_request, (0, 0))

    def wait_out(b, c):
        out_copy(b).wait()
        return c

    lax.fori_loop(0, blocks, wait_out, 0)


def finish(plan, queries, state, near, far, requests):
    block_rows, columns = queries.shape
    heads = columns // HD
    stack = ROWS * heads
    smem = pl.BlockSpec(memory_space=pltpu.SMEM)
    vmem = pl.BlockSpec(memory_space=pltpu.VMEM)
    any_spec = pl.BlockSpec(memory_space=pl.ANY)
    return pl.pallas_call(
        functools.partial(finish_kernel, heads, requests),
        out_shape=jax.ShapeDtypeStruct((block_rows, columns), queries.dtype),
        in_specs=[smem, vmem, vmem, vmem, vmem],
        out_specs=any_spec,
        scratch_shapes=[
            pltpu.VMEM((block_rows // ROWS, ROWS, columns), queries.dtype),
            pltpu.VMEM((stack, HD), jnp.bfloat16),
            pltpu.VMEM((PAGES_MAX // 2, stack, 2 * PAGE), jnp.float32),
            pltpu.SemaphoreType.DMA((block_rows // ROWS,)),
        ],
        compiler_params=pltpu.CompilerParams(vmem_limit_bytes=16 << 20),
        name="finish",
    )(plan, queries, state, near, far)


def in_hbm(x):
    return pltpu.with_memory_space_constraint(x, pltpu.HBM)


def local(queries, fresh_kv, page_pool, page_host, page_slot, prefix_len, fresh_len):
    stores = lax.axis_size("store")
    tps = lax.axis_size("tp")
    requests = page_host.shape[0]
    want, plan = make_plan(page_host, page_slot, prefix_len, fresh_len, stores)
    near, far, state = exchange(
        in_hbm(want), in_hbm(fresh_kv), in_hbm(page_pool), in_hbm(queries), requests, stores, tps
    )
    return finish(plan, queries, state, near, far, requests)


def solution(mesh):
    placed = (
        P("store", "tp"),
        P(None, ("store", "tp"), None),
        P("store", None, None, "tp"),
        P("store", None),
        P("store", None),
        P("store"),
        P("store", None),
    )
    return jax.shard_map(
        local, mesh=mesh, in_specs=placed, out_specs=P("store", "tp"), check_vma=False
    )
```
